32 devices in a mesh: row: 8 (over z, y), col: 4 (over x, core).
Axes of the slice: x: 2, y: 2, z: 4, core: 2. Of those that a mesh axis runs over, the one named last changes fastest.
Arguments:
- examples: bfloat16 [8192, 1024], P('row'), may hold values from -40 to 40
- targets: float32 [8192, 64], P('row'), may hold values from -6 to 6
- landmark_rows: int32 [8192], P('col'), may hold values from 0 to 1023
- ainv: float32 [4, 8, 256, 8192], P(None, 'row', None, 'col'), as said below
- tinv_t: float32 [4, 8, 256, 8192], P(None, 'row', None, 'col'), as said below
Outputs:
- solution: float32 [8192, 64], P('col')
- weights: float32 [8192, 64], P('col')
The draws below stay inside these ranges and needn't reach their ends.
Inputs may be any that keep to these rules, and one draw needn't show every extreme that they name: `landmark_rows`: landmark m is a row of example block ((m mod 2048) // 256); the value is its place within that block. `ainv`: the preconditioner's factor A inverse, in landmark order. `tinv_t`: the preconditioner's factor T inverse, transposed, in landmark order.
All inputs are finite; a program needn't handle non-finite values.
Results may differ from the reference program's by a relative error of at most 0.0003.
Values may be sent and summed in bfloat16 or wider, within the bound.
A program may use at most 128 MiB of HBM per device.

```python
import math
import jax
import jax.numpy as jnp
from jax import lax

D = 1024
M = 8192
C = 64
ROWS_BLK = 1024
ITERS = 2
N = 8192
LT = 2048
LPER = 256
N_ROW = 8
N_COL = 4


def triangle(key, upper):
    first_key, second_key = jax.random.split(key)
    rows_idx = lax.broadcasted_iota(jnp.int32, (M, 1), 0)
    cols_idx = lax.broadcasted_iota(jnp.int32, (1, M), 1)
    spread = jnp.clip(jax.random.normal(first_key, (M, M), jnp.float32), -4.0, 4.0) * (0.6 / math.sqrt(M))
    diagonal = jax.random.uniform(second_key, (1, M), jnp.float32, 0.6, 1.6)
    if upper:
        keep = cols_idx > rows_idx
    else:
        keep = cols_idx < rows_idx
    matrix = jnp.where(keep, spread, 0.0) + jnp.where(cols_idx == rows_idx, diagonal, 0.0)
    return matrix.reshape(N_COL, N_ROW, LPER, M)


def draw_ainv(key, part):
    return triangle(jax.random.fold_in(key, 11), True)


def draw_tinv_t(key, part):
    return triangle(jax.random.fold_in(key, 23), False)


def draw_examples(key, part):
    base = jax.random.fold_in(key, 37)
    id_key, centre_key, spread_key, offset_key, light_key = jax.random.split(base, 5)
    heavy_count = max(2, D // 32)
    cluster_count = max(4, N // 32)
    cluster_ids = jax.random.randint(id_key, (N,), 0, cluster_count)
    centres = jnp.clip(jax.random.normal(centre_key, (cluster_count, heavy_count), jnp.float32), -3.0, 3.0) * 7.0
    spreads = jnp.exp(jax.random.uniform(spread_key, (cluster_count, 1), jnp.float32, math.log(1.2), math.log(4.5)))
    offsets = jnp.clip(jax.random.normal(offset_key, (N, heavy_count), jnp.float32), -3.0, 3.0)
    light = jnp.clip(jax.random.normal(light_key, (N, D - heavy_count), jnp.float32), -4.0, 4.0) * 0.5
    heavy_part = centres[cluster_ids] + spreads[cluster_ids] * offsets
    whole = jnp.concatenate([heavy_part, light], axis=1)
    return whole.astype(jnp.bfloat16)


def plant(drawn, stream_key, least, high):
    spot = [jax.random.randint(jax.random.fold_in(stream_key, axis), (), 0, length) for axis, length in enumerate(drawn.shape)]
    longest = drawn.shape.index(max(drawn.shape))
    neighbour = spot[:longest] + [(spot[longest] + 1) % drawn.shape[longest]] + spot[longest + 1:]
    return drawn.at[tuple(spot)].set(least).at[tuple(neighbour)].set(high)


def block_scale(key, extent, pieces, low, largest):
    gain = 1.0
    for axis_at, shards_of in pieces:
        steps = jax.random.uniform(jax.random.fold_in(jax.random.fold_in(key, 6), axis_at), (shards_of,), jnp.float32, low / len(pieces), largest / len(pieces))
        gain = gain * jnp.repeat(jnp.exp(steps), extent[axis_at] // shards_of).reshape((-1,) + (1,) * (len(extent) - 1 - axis_at))
    return gain


def gaussian(key, extent, deviation, bound, cuts=(), kind=jnp.bfloat16):
    values = deviation * jax.random.normal(key, extent, jnp.float32)
    if cuts:
        values = values * block_scale(key, extent, cuts, -0.22, 0.18)
    return jnp.clip(values, -bound, bound).astype(kind)


def setup_inputs(seed: int = 0) -> dict:
    streams_of = jax.random.split(jax.random.key(seed), 6)
    return {
        "examples": draw_examples(jax.random.fold_in(streams_of[5], 71), 0),
        "targets": gaussian(streams_of[1], (N, C), 1.0, 6.0, ((0, 8),), jnp.float32),
        "landmark_rows": plant(jax.random.randint(streams_of[2], (M,), 0, ROWS_BLK), jax.random.fold_in(streams_of[2], 1), 0, ROWS_BLK - 1).astype(jnp.int32),
        "ainv": draw_ainv(jax.random.fold_in(streams_of[5], 71), 0),
        "tinv_t": draw_tinv_t(jax.random.fold_in(streams_of[5], 71), 0),
    }


LAMBDA = 0.001
EPSILON = 1e-06
HIGHEST = lax.Precision.HIGHEST

def kernel_rows(rows_data, landmarks, sq_lands):
    sq_rows = lax.optimization_barrier(jnp.sum(jnp.square(rows_data.astype(jnp.float32)), axis=1))
    products = lax.dot_general(rows_data, landmarks, (((1,), (1,)), ((), ())), preferred_element_type=jnp.float32)
    return jnp.exp(-(sq_rows[:, None] + sq_lands[None, :] - 2.0 * products) / D)

def contract_rows(matrix, vectors):
    return lax.dot_general(matrix, vectors, (((0,), (0,)), ((), ())), precision=HIGHEST, preferred_element_type=jnp.float32)

def times_matrix(matrix, vectors):
    return jnp.dot(matrix, vectors, precision=HIGHEST, preferred_element_type=jnp.float32)

def reference(examples, targets, landmark_rows, ainv, tinv_t):
    positions = jnp.arange(M, dtype=jnp.int32)
    owners = positions % LT // LPER
    landmarks = examples[(owners * ROWS_BLK + landmark_rows).astype(jnp.int32)]
    sq_lands = lax.optimization_barrier(jnp.sum(jnp.square(landmarks.astype(jnp.float32)), axis=1))
    blocks = examples.reshape(N_ROW, ROWS_BLK, D)

    def one_block(block_data):
        return kernel_rows(block_data, landmarks, sq_lands)
    kernel = lax.map(one_block, blocks).reshape(N, M)
    factor_a = ainv.reshape(M, M)
    factor_t = tinv_t.reshape(M, M)
    kernel_targets = contract_rows(kernel, targets)
    right_side = contract_rows(factor_a, times_matrix(factor_t, kernel_targets)) / math.sqrt(N)
    solution = jnp.zeros((M, C), jnp.float32)
    residual = right_side
    direction = right_side
    norm_now = lax.optimization_barrier(jnp.sum(residual * residual, axis=0))
    for iteration in range(ITERS):
        mixed_in = times_matrix(factor_a, direction)
        lifted = contract_rows(factor_t, mixed_in)
        example_vals = times_matrix(kernel, lifted)
        back = contract_rows(kernel, example_vals)
        lowered = times_matrix(factor_t, back)
        applied = contract_rows(factor_a, lowered / N + LAMBDA * mixed_in)
        step_size = norm_now / lax.optimization_barrier(jnp.sum(direction * applied, axis=0))
        solution = solution + step_size * direction
        residual = residual - step_size * applied
        norm_next = lax.optimization_barrier(jnp.sum(residual * residual, axis=0))
        direction = residual + norm_next / (norm_now + EPSILON) * direction
        norm_now = norm_next
    weights = contract_rows(factor_t, times_matrix(factor_a, solution))
    return (solution, weights)
```

```python
import functools
import math

import jax
import jax.numpy as jnp
from jax import lax
from jax.experimental import pallas as pl
from jax.experimental.pallas import tpu as pltpu
from jax.sharding import PartitionSpec as P

D = 1024
LAMBDA = 0.001
EPSILON = 1e-06
F32 = jnp.float32
BF16 = jnp.bfloat16
MESH = pl.DeviceIdType.MESH


def greet(axis, me, n):
    barrier = pltpu.get_barrier_semaphore()

    def hello(s, carry):
        pl.semaphore_signal(
            barrier, inc=1, device_id={axis: lax.rem(me + s, n)}, device_id_type=MESH
        )
        return carry

    lax.fori_loop(1, n, hello, 0)
    pl.semaphore_wait(barrier, n - 1)


def square_sums(values):
    return jnp.broadcast_to(
        jnp.sum(values * values, axis=1, keepdims=True), (values.shape[0], 128)
    )


def product_kernel(
    axis, n, contract, mat, vec, out, sq_out, send, recv, gath, sq, split,
    s1, r1, s2, r2, s3, r3,
):
    me = lax.axis_index(axis)
    c = vec.shape[0]
    w = send.shape[2]

    def to_peer(src, dst, ssem, rsem, peer):
        return pltpu.make_async_remote_copy(
            src_ref=src, dst_ref=dst, send_sem=ssem, recv_sem=rsem,
            device_id={axis: peer}, device_id_type=MESH,
        )

    values = vec[...]
    high = values.astype(BF16)
    split[0:c, :] = high
    split[c:, :] = (values - high.astype(F32)).astype(BF16)
    sq[me] = square_sums(values)
    greet(axis, me, n)

    def chunk_product(j):
        if contract:
            start = j * w if isinstance(j, int) else pl.multiple_of(j * w, 128)
            m = mat[:, pl.ds(start, w)]
            dims = (((1,), (0,)), ((), ()))
        else:
            start = j * w if isinstance(j, int) else pl.multiple_of(j * w, 8)
            m = mat[pl.ds(start, w), :]
            dims = (((1,), (1,)), ((), ()))
        m_high = m.astype(BF16)
        m_low = (m - m_high.astype(F32)).astype(BF16)
        both = lax.dot_general(split[...], m_high, dims, preferred_element_type=F32)
        rest = lax.dot_general(split[0:c, :], m_low, dims, preferred_element_type=F32)
        return both[0:c] + (both[c:] + rest)

    aligned = w % 128 == 0
    if not aligned:
        for j in range(n):
            send[j] = chunk_product(j)

    def first(s, carry):
        peer = lax.rem(me + s, n)
        if aligned:
            send[peer] = chunk_product(peer)
        to_peer(send.at[peer], recv.at[s], s1.at[s], r1.at[s], peer).start()
        to_peer(sq.at[me], sq.at[me], s3.at[s], r3.at[s], peer).start()
        return carry

    lax.fori_loop(1, n, first, 0)
    if aligned:
        send[me] = chunk_product(me)

    def gather_in(s, total):
        to_peer(send.at[0], recv.at[s], s1.at[s], r1.at[s], lax.rem(me + s, n)).wait_recv()
        return total + recv[s]

    gath[me] = lax.fori_loop(1, n, gather_in, send[me])

    def second(s, carry):
        peer = lax.rem(me + s, n)
        to_peer(gath.at[me], gath.at[me], s2.at[s], r2.at[s], peer).start()
        return carry

    lax.fori_loop(1, n, second, 0)

    def finish(s, carry):
        source = lax.rem(me + n - s, n)
        to_peer(sq.at[me], sq.at[source], s3.at[s], r3.at[s], lax.rem(me + s, n)).wait()
        to_peer(gath.at[me], gath.at[source], s2.at[s], r2.at[s], lax.rem(me + s, n)).wait()
        to_peer(send.at[0], recv.at[s], s1.at[s], r1.at[s], lax.rem(me + s, n)).wait_send()
        return carry

    lax.fori_loop(1, n, finish, 0)
    total = sq[0]
    for j in range(1, n):
        total = total + sq[j]
    sq_out[...] = total
    for j in range(n):
        out[:, j * w : (j + 1) * w] = gath[j]


def product(axis, contract, ident, mat, vec):
    n = lax.axis_size(axis)
    c = vec.shape[0]
    length = mat.shape[1] if contract else mat.shape[0]
    depth = mat.shape[0] if contract else mat.shape[1]
    w = length // n
    vmem = pl.BlockSpec(memory_space=pltpu.VMEM)
    out, sq = pl.pallas_call(
        functools.partial(product_kernel, axis, n, contract),
        out_shape=(
            jax.ShapeDtypeStruct((c, length), F32),
            jax.ShapeDtypeStruct((c, 128), F32),
        ),
        in_specs=[vmem, vmem],
        out_specs=(vmem, vmem),
        scratch_shapes=[
            pltpu.VMEM((n, c, w), F32),
            pltpu.VMEM((n, c, w), F32),
            pltpu.VMEM((n, c, w), F32),
            pltpu.VMEM((n, c, 128), F32),
            pltpu.VMEM((2 * c, depth), BF16),
        ]
        + [pltpu.SemaphoreType.DMA((n,))] * 6,
        compiler_params=pltpu.CompilerParams(
            collective_id=ident, has_side_effects=True, vmem_limit_bytes=48 * 2**20
        ),
    )(mat, vec)
    return out, sq[:, 0:1]


def square_kernel(axis, n, vec, sq_out, sq, s3, r3):
    me = lax.axis_index(axis)
    sq[me] = square_sums(vec[...])
    greet(axis, me, n)

    def copy(s, slot, peer):
        return pltpu.make_async_remote_copy(
            src_ref=sq.at[me], dst_ref=sq.at[slot], send_sem=s3.at[s], recv_sem=r3.at[s],
            device_id={axis: peer}, device_id_type=MESH,
        )

    def start(s, carry):
        copy(s, me, lax.rem(me + s, n)).start()
        return carry

    def finish(s, carry):
        copy(s, lax.rem(me + n - s, n), lax.rem(me + s, n)).wait()
        return carry

    lax.fori_loop(1, n, start, 0)
    lax.fori_loop(1, n, finish, 0)
    total = sq[0]
    for j in range(1, n):
        total = total + sq[j]
    sq_out[...] = total


def square_total(axis, ident, vec):
    n = lax.axis_size(axis)
    c = vec.shape[0]
    vmem = pl.BlockSpec(memory_space=pltpu.VMEM)
    return pl.pallas_call(
        functools.partial(square_kernel, axis, n),
        out_shape=jax.ShapeDtypeStruct((c, 128), F32),
        in_specs=[vmem],
        out_specs=vmem,
        scratch_shapes=[pltpu.VMEM((n, c, 128), F32)] + [pltpu.SemaphoreType.DMA((n,))] * 2,
        compiler_params=pltpu.CompilerParams(collective_id=ident, has_side_effects=True),
    )(vec)[:, 0:1]


def kernel_tile(rows_data, landmarks):
    sq_lands = jnp.sum(jnp.square(landmarks.astype(F32)), axis=1)
    sq_rows = jnp.sum(jnp.square(rows_data.astype(F32)), axis=1)
    products = lax.dot_general(
        rows_data, landmarks, (((1,), (1,)), ((), ())), preferred_element_type=F32
    )
    return jnp.exp(-(sq_rows[:, None] + sq_lands[None, :] - 2.0 * products) / D)


def shards(examples, targets, landmark_rows, ainv, tinv_t):
    row_count = lax.axis_size("row")
    total_rows = examples.shape[0] * row_count
    tile_width = landmark_rows.shape[0]
    owned_count = tile_width // row_count
    first_owned = lax.axis_index("row") * owned_count
    owned_ids = lax.dynamic_slice_in_dim(landmark_rows, first_owned, owned_count, 0)
    owned = jnp.take(examples, owned_ids, axis=0)
    landmarks = lax.all_gather(owned, "row", axis=0, tiled=True)
    kernel = kernel_tile(examples, landmarks)
    factor_a = ainv.reshape(-1, tile_width)
    factor_t = tinv_t.reshape(-1, tile_width)

    kernel_back = functools.partial(product, "row", True, 0, kernel)
    kernel_on = functools.partial(product, "col", False, 1, kernel)
    factor_back = functools.partial(product, "row", True, 2)
    factor_on = functools.partial(product, "col", False, 3)

    kernel_targets, _ = kernel_back(targets.T)
    mixed, _ = factor_on(factor_t, kernel_targets)
    right_side, _ = factor_back(factor_a, mixed)
    right_side = right_side / math.sqrt(total_rows)

    mixed_0, norm_0 = factor_on(factor_a, right_side)
    lifted_0, mixed_sq = factor_back(factor_t, mixed_0)
    example_vals, _ = kernel_on(lifted_0)
    back, vals_sq = kernel_back(example_vals)
    step_0 = norm_0 / (vals_sq / total_rows + LAMBDA * mixed_sq)
    lowered, _ = factor_on(factor_t, back)
    applied, _ = factor_back(factor_a, lowered / total_rows + LAMBDA * mixed_0)
    residual = right_side - step_0 * applied

    mixed_r, norm_1 = factor_on(factor_a, residual)
    ratio = norm_1 / (norm_0 + EPSILON)
    direction = residual + ratio * right_side
    lifted_1, mixed_sq = factor_back(factor_t, mixed_r + ratio * mixed_0)
    example_vals, _ = kernel_on(lifted_1)
    vals_sq = square_total("row", 4, example_vals)
    step_1 = norm_1 / (vals_sq / total_rows + LAMBDA * mixed_sq)
    solution = step_0 * right_side + step_1 * direction
    weights = step_0 * lifted_0 + step_1 * lifted_1
    return (solution.T, weights.T)


def solution(mesh):
    return jax.shard_map(
        shards,
        mesh=mesh,
        in_specs=(
            P("row", None),
            P("row", None),
            P("col"),
            P(None, "row", None, "col"),
            P(None, "row", None, "col"),
        ),
        out_specs=(P("col", None), P("col", None)),
        check_vma=False,
    )
```
